32 devices in a mesh: seq: 4 (over x, core), fsdp: 8 (over z, y).
Axes of the slice: x: 2, y: 2, z: 4, core: 2. Of those that a mesh axis runs over, the one named last changes fastest.
Arguments:
- query_in: bfloat16 [8, 512, 3072], P('fsdp', 'seq'), may hold values from -10 to 10
- key_in: bfloat16 [8, 512, 3072], P('fsdp', 'seq'), may hold values from -10 to 10
- value_in: bfloat16 [8, 512, 3072], P('fsdp', 'seq'), may hold values from -6 to 6
- positions: int32 [8, 512], P('fsdp', 'seq'), may hold values from 0 to 1023, as said below
- grad_out: bfloat16 [8, 512, 4096], P('fsdp', 'seq'), may hold values from -12 to 12
- out_weight: bfloat16 [3072, 4096], P('seq', 'fsdp'), may hold values from -0.109375 to 0.109375
Outputs:
- grad_query: bfloat16 [8, 512, 3072], P('fsdp', 'seq')
- grad_key: bfloat16 [8, 512, 3072], P('fsdp', 'seq')
- grad_value: bfloat16 [8, 512, 3072], P('fsdp', 'seq')
- grad_weight: float32 [3072, 4096], P('seq', 'fsdp')
The draws below stay inside these ranges and needn't reach their ends.
Inputs may be any that keep to these rules, and one draw needn't show every extreme that they name: Within a clip the positions rise strictly; the first is 0 and the last is 1023.
All inputs are finite; a program needn't handle non-finite values.
Results may differ from the reference program's by a relative error of at most 0.004.
The reference program's roundings to bfloat16 on the way (of `rot_query`, `rot_key`, `probs_low`, `attended`, `grad_attended` and `grad_scores`) count: a program that leaves them out, or rounds other values in their place, can miss the bound.
Values may be sent and summed in bfloat16 or wider, within the bound.
No kernel may reach another device: no remote copies, remote signals or barrier semaphores. Data moves between devices by JAX's collectives and lax.ppermute only.
A program may use at most 128 MiB of HBM per device.

```python
import jax
import jax.numpy as jnp
from jax import lax

D = 4096
HEADS = 24
HD = 128
LENGTH = 512
CLIPS = 8


def base_draw(key):
    full_dims = (CLIPS, LENGTH, HEADS, HD)
    return jnp.clip(1.4 * jax.random.normal(key, full_dims, jnp.float32), -8.4, 8.4)


def draw_query_in(key, part):
    base = base_draw(jax.random.fold_in(key, 11))
    return base.reshape(CLIPS, LENGTH, HEADS * HD).astype(jnp.bfloat16)


def draw_key_in(key, part):
    base = base_draw(jax.random.fold_in(key, 13))
    return base.reshape(CLIPS, LENGTH, HEADS * HD).astype(jnp.bfloat16)


def draw_positions(key, part):
    inner = 2 * LENGTH - 2

    def one_clip(clip_key):
        order = jax.random.permutation(clip_key, inner) + 1
        chosen = jnp.sort(order[:LENGTH - 2])
        return jnp.concatenate([jnp.zeros((1,), jnp.int32), chosen.astype(jnp.int32), jnp.full((1,), 2 * LENGTH - 1, jnp.int32)])
    clip_keys = jax.random.split(jax.random.fold_in(key, 17), CLIPS)
    return jax.vmap(one_clip)(clip_keys).astype(jnp.int32)


def raised(result, key, source, target, parts, factor):
    owner, partner = [(jnp.arange(result.shape[axis_at]) // (result.shape[axis_at] // parts)).reshape([-1 if axis == axis_at else 1 for axis in range(result.ndim)]) for axis_at in (source, target)]
    chosen = jax.random.permutation(key, parts)[partner]
    strong = (owner == chosen) | (owner == (partner + parts // 2) % parts)
    return jnp.where(strong, factor * result, result)


def steps_of(own_key, extent, cuts, low, largest):
    def one(position, parts):
        steps = jax.random.uniform(jax.random.fold_in(jax.random.fold_in(own_key, 6), position), (parts,), jnp.float32, low / len(cuts), largest / len(cuts))
        return jnp.repeat(jnp.exp(steps), extent[position] // parts).reshape((-1,) + (1,) * (len(extent) - position - 1))

    loudness = one(*cuts[0])
    for cut in cuts[1:]:
        loudness = loudness * one(*cut)
    return loudness


def scatter_about(rng, extent, deviation, most, cuts=(), kind=jnp.bfloat16):
    level = steps_of(rng, extent, cuts, -0.22, 0.18) if cuts else 1.0
    drawn = jax.random.normal(rng, extent, jnp.float32) * deviation * level
    return jnp.minimum(jnp.maximum(drawn, -most), most).astype(kind)


def heavy_noise(stream_key, shape, deviation, most, cuts, heavy, kind=jnp.bfloat16):
    drawn = deviation * jax.random.normal(stream_key, shape, jnp.float32)
    if cuts:
        drawn = drawn * steps_of(stream_key, shape, cuts, -0.22, 0.18)
    return jnp.clip(raised(drawn, jax.random.fold_in(stream_key, 3), *heavy), -most, most).astype(kind)


def setup_inputs(seed: int = 0) -> dict:
    streams_of = jax.random.split(jax.random.key(seed), 7)
    query_in = draw_query_in(jax.random.fold_in(streams_of[6], 71), 0)
    key_in = draw_key_in(jax.random.fold_in(streams_of[6], 71), 0)
    value_in = scatter_about(streams_of[2], (CLIPS, LENGTH, HEADS * HD), 1.0, 6.0, ((0, 8), (1, 4)))
    positions = draw_positions(jax.random.fold_in(streams_of[6], 71), 0)
    grad_out = heavy_noise(streams_of[4], (CLIPS, LENGTH, D), 2.0, 12.0, ((0, 8), (1, 4)), (0, 2, 8, 2.0))
    out_weight = scatter_about(streams_of[5], (HEADS * HD, D), (HEADS * HD) ** -0.5, 0.109375, ((0, 4), (1, 8)))
    return dict(query_in=query_in, key_in=key_in, value_in=value_in, positions=positions, grad_out=grad_out, out_weight=out_weight)


def rotary_tables(positions, head_dim):
    half_dim = head_dim // 2
    frequency = 10000.0 ** (-2.0 * jnp.arange(half_dim, dtype=jnp.float32) / head_dim)
    angles = positions.astype(jnp.float32)[:, None] * frequency[None, :]
    return jnp.cos(angles), jnp.sin(angles)


def rotate(field, cosine_tab, sine_tab):
    half_dim = field.shape[-1] // 2
    front_half = field[..., :half_dim]
    back_half = field[..., half_dim:]
    cosine_b = cosine_tab[:, None, :]
    sine_b = sine_tab[:, None, :]
    return jnp.concatenate([front_half * cosine_b - back_half * sine_b, front_half * sine_b + back_half * cosine_b], axis=-1)


def unrotate(field, cosine_tab, sine_tab):
    half_dim = field.shape[-1] // 2
    front_half = field[..., :half_dim]
    back_half = field[..., half_dim:]
    cosine_b = cosine_tab[:, None, :]
    sine_b = sine_tab[:, None, :]
    return jnp.concatenate([front_half * cosine_b + back_half * sine_b, back_half * cosine_b - front_half * sine_b], axis=-1)


def head_grads(inputs):
    query_head, key_head, value_head, grad_head = inputs
    factor = HD ** -0.5
    scores = jnp.dot(query_head, key_head.T, preferred_element_type=jnp.float32)
    row_top = jnp.max(scores, axis=1, keepdims=True)
    expo = jnp.exp(scores - row_top)
    attn_probs = expo / jnp.sum(expo, axis=1, keepdims=True)
    probs_low = attn_probs.astype(jnp.bfloat16)
    attended = jnp.dot(probs_low, value_head, preferred_element_type=jnp.float32).astype(jnp.bfloat16)
    grad_value = jnp.dot(probs_low.T, grad_head, preferred_element_type=jnp.float32).astype(jnp.bfloat16)
    grad_probs = jnp.dot(grad_head, value_head.T, preferred_element_type=jnp.float32)
    row_delta = jnp.sum(attn_probs * grad_probs, axis=1, keepdims=True)
    grad_scores = (attn_probs * (grad_probs - row_delta)).astype(jnp.bfloat16)
    rot_grad_query = (jnp.dot(grad_scores, key_head, preferred_element_type=jnp.float32) * factor).astype(jnp.bfloat16)
    rot_grad_key = jnp.dot(grad_scores.T, query_head, preferred_element_type=jnp.float32).astype(jnp.bfloat16)
    return attended, grad_value, rot_grad_query, rot_grad_key


def reference(query_in, key_in, value_in, positions, grad_out, out_weight):
    factor = HD ** -0.5

    def clip_step(running, inputs):
        query_clip, key_clip, value_clip, place_clip, grad_clip = inputs
        cosine_tab, sine_tab = rotary_tables(place_clip, HD)
        rot_query = (rotate(query_clip.astype(jnp.float32).reshape(LENGTH, HEADS, HD), cosine_tab, sine_tab) * factor).astype(jnp.bfloat16)
        rot_key = rotate(key_clip.astype(jnp.float32).reshape(LENGTH, HEADS, HD), cosine_tab, sine_tab).astype(jnp.bfloat16)
        value_rows = value_clip.reshape(LENGTH, HEADS, HD)
        grad_attended = jnp.dot(grad_clip, out_weight.T, preferred_element_type=jnp.float32).astype(jnp.bfloat16)
        grad_attended = grad_attended.reshape(LENGTH, HEADS, HD)
        attended, grad_value, rot_grad_query, rot_grad_key = lax.map(head_grads, (rot_query.transpose(1, 0, 2), rot_key.transpose(1, 0, 2), value_rows.transpose(1, 0, 2), grad_attended.transpose(1, 0, 2)))
        attended_flat = attended.transpose(1, 0, 2).reshape(LENGTH, HEADS * HD)
        running = running + jnp.dot(attended_flat.T, grad_clip, preferred_element_type=jnp.float32)
        grad_query = unrotate(rot_grad_query.transpose(1, 0, 2).astype(jnp.float32), cosine_tab, sine_tab).astype(jnp.bfloat16)
        grad_key = unrotate(rot_grad_key.transpose(1, 0, 2).astype(jnp.float32), cosine_tab, sine_tab).astype(jnp.bfloat16)
        grad_value = grad_value.transpose(1, 0, 2)
        return running, (grad_query.reshape(LENGTH, HEADS * HD), grad_key.reshape(LENGTH, HEADS * HD), grad_value.reshape(LENGTH, HEADS * HD))

    start_sum = jnp.zeros((HEADS * HD, D), jnp.float32)
    grad_weight, outputs = lax.scan(clip_step, start_sum, (query_in, key_in, value_in, positions, grad_out))
    return outputs[0], outputs[1], outputs[2], grad_weight
```

```python
import jax
import jax.numpy as jnp
from jax import lax
from jax.experimental import pallas as pl
from jax.experimental.pallas import tpu as pltpu
from jax.sharding import PartitionSpec as P


HD = 128
CHUNKS = 3
BF = jnp.bfloat16
F32 = jnp.float32
VMEM_LIMIT = 16 * 1024 * 1024


NT = (((1,), (1,)), ((), ()))
TN = (((0,), (0,)), ((), ()))
NN = (((1,), (0,)), ((), ()))


def mm(a, b, dims):
    return lax.dot_general(a, b, dims, preferred_element_type=F32)


def call(kernel, outs, flops, nbytes, **kw):
    return pl.pallas_call(
        kernel,
        out_shape=outs,
        compiler_params=pltpu.CompilerParams(vmem_limit_bytes=VMEM_LIMIT),
        cost_estimate=pl.CostEstimate(flops=int(flops), bytes_accessed=int(nbytes), transcendentals=0),
        **kw,
    )


def whole():
    return pl.BlockSpec(memory_space=pltpu.VMEM)


def smem():
    return pl.BlockSpec(memory_space=pltpu.SMEM)


def bits_of(n):
    assert n & (n - 1) == 0
    return [1 << i for i in range(n.bit_length() - 1)]


def split_columns(grad, blocks, order, pair):
    tok, width = grad.shape
    step = width // blocks

    def kernel(at, g, own, other):
        for j, m in enumerate(order):
            for base, out in ((at[1], own), (at[1] ^ pair, other)):
                start = pl.multiple_of((base ^ m) * step, step)
                out[:, j * step : (j + 1) * step] = g[:, pl.ds(start, step)]

    def run(at):
        shape = jax.ShapeDtypeStruct((tok, width // 2), grad.dtype)
        return call(
            kernel, (shape, shape), 0, 4 * grad.size,
            in_specs=[smem(), whole()], out_specs=(whole(), whole()),
        )(at, grad)

    return run


def cut_heads(query, key, value, cosine, sine, at, seq, sizes):
    tok, width = query.shape
    rows = width // seq
    factor = HD ** (-0.5)

    def kernel(at_ref, q, k, v, cos, sin, *outs):
        c, s = cos[...], sin[...]
        for part in range(seq):
            start = (at_ref[0] ^ part) * rows
            head = 0
            for j, size in enumerate(sizes):
                out = outs[j * seq + part]
                for h in range(size):
                    cols = pl.ds(pl.multiple_of(start + head * HD, HD), HD)
                    x = q[:, cols].astype(F32)
                    out[h, 0] = ((x * c + pltpu.roll(x, HD // 2, 1) * s) * factor).astype(BF)
                    x = k[:, cols].astype(F32)
                    out[h, 1] = (x * c + pltpu.roll(x, HD // 2, 1) * s).astype(BF)
                    out[h, 2] = v[:, cols]
                    head += 1

    outs = [jax.ShapeDtypeStruct((n, 3, tok, HD), BF) for n in sizes for _ in range(seq)]
    res = call(
        kernel, outs, 0, 12 * query.size,
        in_specs=[smem()] + [whole()] * 5, out_specs=[whole()] * len(outs),
    )(at, query, key, value, cosine, sine)
    return [list(res[j * seq : (j + 1) * seq]) for j in range(len(sizes))]


def gathered(refs, head, which):
    return jnp.concatenate([r[head, which] for r in refs], axis=0)


def probs_of(query, key):
    scores = mm(key, query, NT)
    expo = jnp.exp(scores - jnp.max(scores, axis=0, keepdims=True))
    return expo * (1.0 / jnp.sum(expo, axis=0, keepdims=True))


def attend(parts):
    count, _, tok, _ = parts[0].shape
    length = tok * len(parts)

    def kernel(*refs):
        ins, out = refs[:-1], refs[-1]
        for h in range(count):
            low = probs_of(gathered(ins, h, 0), gathered(ins, h, 1)).astype(BF)
            out[h * HD : (h + 1) * HD] = mm(gathered(ins, h, 2), low, TN).astype(BF)

    return call(
        kernel, jax.ShapeDtypeStruct((count * HD, length), BF),
        4 * count * length * length * HD, 8 * count * length * HD,
        in_specs=[whole()] * len(parts), out_specs=whole(),
    )(*parts)


def attend_back(parts, mine, theirs):
    count, _, tok, _ = parts[0].shape
    length = tok * len(parts)
    factor = HD ** (-0.5)
    seq = len(parts)

    def kernel(*refs):
        ins, (a, b), outs = refs[:seq], refs[seq : seq + 2], refs[seq + 2 :]
        for h in range(count):
            cols = slice(h * HD, (h + 1) * HD)
            query, key, value = (gathered(ins, h, i) for i in range(3))
            grad = (a[:, cols] + b[:, cols].astype(F32)).astype(BF)
            probs = probs_of(query, key)
            grad_value = mm(probs.astype(BF), grad, NN)
            grad_probs = mm(value, grad, NT)
            delta = jnp.sum(probs * grad_probs, axis=0, keepdims=True)
            grad_scores = (probs * (grad_probs - delta)).astype(BF)
            grad_key = mm(grad_scores, query, NN)
            grad_query = (mm(key, grad_scores, TN) * factor).T
            for i, out in enumerate(outs):
                at = slice(i * tok, (i + 1) * tok)
                out[h, 0] = grad_query[at].astype(BF)
                out[h, 1] = grad_key[at].astype(BF)
                out[h, 2] = grad_value[at].astype(BF)

    return list(call(
        kernel, [jax.ShapeDtypeStruct(parts[0].shape, BF)] * seq,
        12 * count * length * length * HD, 20 * count * length * HD,
        in_specs=[whole()] * (seq + 2), out_specs=[whole()] * seq,
    )(*parts, mine, theirs))


def rows_of(refs, cols):
    return jnp.concatenate([r[:, cols] for r in refs], axis=0)


def project_back(grads, weights, kind):
    count, blocks = len(grads), len(weights)
    tok, width = grads[0].shape
    rows, step = weights[0].shape
    total = tok * count
    half = total // 2

    def kernel(*refs):
        grad_refs, weight_refs = refs[:count], refs[count : count + blocks]
        mine, theirs = refs[count + blocks :]
        acc = None
        for j in range(blocks):
            left = rows_of(grad_refs, slice(j * step, (j + 1) * step))
            term = mm(left, weight_refs[j][...], NT)
            acc = term if acc is None else acc + term
        mine[...] = acc[:half]
        theirs[...] = acc[half:].astype(kind)

    return call(
        kernel,
        (jax.ShapeDtypeStruct((half, rows), F32), jax.ShapeDtypeStruct((half, rows), kind)),
        2 * total * width * rows, 2 * total * width + 2 * rows * width + 6 * half * rows,
        in_specs=[whole()] * (count + blocks), out_specs=(whole(), whole()),
    )(*grads, *weights)


def weight_terms(grads, mine, theirs, types):
    count, blocks = len(grads), len(types)
    tok, width = grads[0].shape
    rows, _ = mine.shape
    step = width // blocks
    total = tok * count

    def kernel(*refs):
        grad_refs, (a, b), outs = refs[:count], refs[count : count + 2], refs[count + 2 :]
        left = jnp.concatenate([a[...], b[...]], axis=1)
        for j in range(blocks):
            right = rows_of(grad_refs, slice(j * step, (j + 1) * step))
            outs[j][...] = mm(left, right, NN).astype(outs[j].dtype)

    return list(call(
        kernel, [jax.ShapeDtypeStruct((rows, step), t) for t in types],
        2 * total * width * rows, 2 * total * width + 4 * rows * width,
        in_specs=[whole()] * (count + 2), out_specs=[whole()] * blocks,
    )(*grads, mine, theirs))


def join_heads(chunks, cosine, sine, at, seq, sizes):
    tok = cosine.shape[0]
    rows = sum(sizes) * HD
    width = rows * seq

    def kernel(at_ref, cos, sin, *refs):
        ins, outs = refs[:-3], refs[-3:]
        c, s = cos[...], sin[...]
        for part in range(seq):
            start = (at_ref[0] ^ part) * rows
            head = 0
            for j, size in enumerate(sizes):
                src = ins[j * seq + part]
                for h in range(size):
                    cols = pl.ds(pl.multiple_of(start + head * HD, HD), HD)
                    for i in range(2):
                        x = src[h, i].astype(F32)
                        outs[i][:, cols] = (x * c - pltpu.roll(x, HD // 2, 1) * s).astype(BF)
                    outs[2][:, cols] = src[h, 2]
                    head += 1

    flat = [x for chunk in chunks for x in chunk]
    shape = jax.ShapeDtypeStruct((tok, width), BF)
    return call(
        kernel, (shape, shape, shape), 0, 12 * tok * width,
        in_specs=[smem()] + [whole()] * (2 + len(flat)), out_specs=(whole(),) * 3,
    )(at, cosine, sine, *flat)


def rotary_tables(positions):
    half = HD // 2
    frequency = 10000.0 ** (-2.0 * jnp.arange(half, dtype=F32) / HD)
    angles = positions.astype(F32)[:, None] * frequency[None, :]
    cosine, sine = jnp.cos(angles), jnp.sin(angles)
    return jnp.concatenate([cosine, cosine], 1), jnp.concatenate([-sine, sine], 1)


def shards(seq, fsdp, query_in, key_in, value_in, positions, grad_out, out_weight):
    query, key, value, grad = query_in[0], key_in[0], value_in[0], grad_out[0]
    seq_bits, clip_bits = bits_of(seq), bits_of(fsdp)
    pair = clip_bits[0]
    rest = [b for b in clip_bits if b != pair]
    order = [0]
    for bit in reversed(rest):
        order += [m | bit for m in order]
    heads = query.shape[1] // HD // seq
    chunks = min(CHUNKS, heads)
    sizes = [heads // chunks + (j < heads % chunks) for j in range(chunks)]
    edges = [sum(sizes[:j]) * HD for j in range(chunks + 1)]

    at = jnp.stack([lax.axis_index("seq"), lax.axis_index("fsdp")]).astype(jnp.int32)

    def send(x, axis, bit):
        n = {"seq": seq, "fsdp": fsdp}[axis]
        return lax.ppermute(x, axis, [(i, i ^ bit) for i in range(n)])

    split = split_columns(grad, fsdp, order, pair)
    own, other = split(at)
    grads = [{0: own}, {0: send(other, "fsdp", pair)}]
    for held in grads:
        for bit in reversed(seq_bits):
            for m in list(held):
                held[m | bit] = send(held[m], "seq", bit)
    sides = [held[m] for held in grads for m in range(seq)]

    weights = []
    for j in range(chunks):
        held = {0: out_weight[edges[j] : edges[j + 1]]}
        for bit in reversed(rest):
            for m in list(held):
                held[m | bit] = send(held[m], "fsdp", bit)
        weights.append([held[m] for m in order])

    cosine, sine = rotary_tables(positions[0])
    parts = cut_heads(query, key, value, cosine, sine, at, seq, sizes)
    parts = [[p if m == 0 else send(p, "seq", m) for m, p in enumerate(c)] for c in parts]

    types = [BF if rest and m & rest[0] else F32 for m in order]
    back, grad_weight = [], []
    for j in range(chunks):
        mine = attend(parts[j])
        theirs = send(mine, "fsdp", pair)
        terms = dict(zip(order, weight_terms(sides, mine, theirs, types)))
        for bit in rest:
            for m in [m for m in order if m & bit and m in terms]:
                got = send(terms.pop(m).astype(BF), "fsdp", bit)
                terms[m ^ bit] = terms[m ^ bit] + got.astype(F32)
        grad_weight.append(terms[0])

        kind = F32
        near, far = project_back(sides, weights[j], kind)
        far = send(far, "fsdp", pair)
        grads_back = attend_back(parts[j], near, far)
        back.append([g if m == 0 else send(g, "seq", m) for m, g in enumerate(grads_back)])

    outs = join_heads(back, cosine, sine, at, seq, sizes)
    return (*(o[None] for o in outs), jnp.concatenate(grad_weight, 0))


def solution(mesh):
    tokens = P("fsdp", "seq", None)

    def body(*args):
        return shards(mesh.shape["seq"], mesh.shape["fsdp"], *args)

    return jax.shard_map(
        body,
        mesh=mesh,
        in_specs=(tokens, tokens, tokens, P("fsdp", "seq"), tokens, P("seq", "fsdp")),
        out_specs=(tokens, tokens, tokens, P("seq", "fsdp")),
        check_vma=False,
    )
```

```python
import jax
import jax.numpy as jnp
from jax import lax
from jax.experimental import pallas as pl
from jax.experimental.pallas import tpu as pltpu
from jax.sharding import PartitionSpec as P


HD = 128
CHUNKS = 3
BF = jnp.bfloat16
F32 = jnp.float32
VMEM_LIMIT = 16 * 1024 * 1024


NT = (((1,), (1,)), ((), ()))
TN = (((0,), (0,)), ((), ()))
NN = (((1,), (0,)), ((), ()))


def mm(a, b, dims):
    return lax.dot_general(a, b, dims, preferred_element_type=F32)


def call(kernel, outs, flops, nbytes, **kw):
    return pl.pallas_call(
        kernel,
        out_shape=outs,
        compiler_params=pltpu.CompilerParams(vmem_limit_bytes=VMEM_LIMIT),
        cost_estimate=pl.CostEstimate(flops=int(flops), bytes_accessed=int(nbytes), transcendentals=0),
        **kw,
    )


def whole():
    return pl.BlockSpec(memory_space=pltpu.VMEM)


def smem():
    return pl.BlockSpec(memory_space=pltpu.SMEM)


def bits_of(n):
    assert n & (n - 1) == 0
    return [1 << i for i in range(n.bit_length() - 1)]


def split_columns(grad, blocks, order, pair):
    tok, width = grad.shape
    step = width // blocks

    def kernel(at, g, own, other):
        for j, m in enumerate(order):
            for base, out in ((at[1], own), (at[1] ^ pair, other)):
                start = pl.multiple_of((base ^ m) * step, step)
                out[:, j * step : (j + 1) * step] = g[:, pl.ds(start, step)]

    def run(at):
        shape = jax.ShapeDtypeStruct((tok, width // 2), grad.dtype)
        return call(
            kernel, (shape, shape), 0, 4 * grad.size,
            in_specs=[smem(), whole()], out_specs=(whole(), whole()),
        )(at, grad)

    return run


def cut_heads(query, key, value, cosine, sine, at, seq, sizes):
    tok, width = query.shape
    rows = width // seq
    factor = HD ** (-0.5)

    def kernel(at_ref, q, k, v, cos, sin, *outs):
        c, s = cos[...], sin[...]
        for part in range(seq):
            start = (at_ref[0] ^ part) * rows
            head = 0
            for j, size in enumerate(sizes):
                out = outs[j * seq + part]
                for h in range(size):
                    cols = pl.ds(pl.multiple_of(start + head * HD, HD), HD)
                    x = q[:, cols].astype(F32)
                    out[h, 0] = ((x * c + pltpu.roll(x, HD // 2, 1) * s) * factor).astype(BF)
                    x = k[:, cols].astype(F32)
                    out[h, 1] = (x * c + pltpu.roll(x, HD // 2, 1) * s).astype(BF)
                    out[h, 2] = v[:, cols]
                    head += 1

    outs = [jax.ShapeDtypeStruct((n, 3, tok, HD), BF) for n in sizes for _ in range(seq)]
    res = call(
        kernel, outs, 0, 12 * query.size,
        in_specs=[smem()] + [whole()] * 5, out_specs=[whole()] * len(outs),
    )(at, query, key, value, cosine, sine)
    return [list(res[j * seq : (j + 1) * seq]) for j in range(len(sizes))]


def gathered(refs, head, which):
    return jnp.concatenate([r[head, which] for r in refs], axis=0)


def probs_of(query, key):
    scores = mm(key, query, NT)
    expo = jnp.exp(scores - jnp.max(scores, axis=0, keepdims=True))
    return expo * (1.0 / jnp.sum(expo, axis=0, keepdims=True))


def attend(parts):
    count, _, tok, _ = parts[0].shape
    length = tok * len(parts)

    def kernel(*refs):
        ins, out = refs[:-1], refs[-1]
        for h in range(count):
            low = probs_of(gathered(ins, h, 0), gathered(ins, h, 1)).astype(BF)
            out[h * HD : (h + 1) * HD] = mm(gathered(ins, h, 2), low, TN).astype(BF)

    return call(
        kernel, jax.ShapeDtypeStruct((count * HD, length), BF),
        4 * count * length * length * HD, 8 * count * length * HD,
        in_specs=[whole()] * len(parts), out_specs=whole(),
    )(*parts)


def attend_back(parts, mine, theirs):
    count, _, tok, _ = parts[0].shape
    length = tok * len(parts)
    factor = HD ** (-0.5)
    seq = len(parts)

    def kernel(*refs):
        ins, (a, b), outs = refs[:seq], refs[seq : seq + 2], refs[seq + 2 :]
        for h in range(count):
            cols = slice(h * HD, (h + 1) * HD)
            query, key, value = (gathered(ins, h, i) for i in range(3))
            grad = (a[:, cols] + b[:, cols].astype(F32)).astype(BF)
            probs = probs_of(query, key)
            grad_value = mm(probs.astype(BF), grad, NN)
            grad_probs = mm(value, grad, NT)
            delta = jnp.sum(probs * grad_probs, axis=0, keepdims=True)
            grad_scores = (probs * (grad_probs - delta)).astype(BF)
            grad_key = mm(grad_scores, query, NN)
            grad_query = (mm(key, grad_scores, TN) * factor).T
            for i, out in enumerate(outs):
                at = slice(i * tok, (i + 1) * tok)
                out[h, 0] = grad_query[at].astype(BF)
                out[h, 1] = grad_key[at].astype(BF)
                out[h, 2] = grad_value[at].astype(BF)

    return list(call(
        kernel, [jax.ShapeDtypeStruct(parts[0].shape, BF)] * seq,
        12 * count * length * length * HD, 20 * count * length * HD,
        in_specs=[whole()] * (seq + 2), out_specs=[whole()] * seq,
    )(*parts, mine, theirs))


def rows_of(refs, cols):
    return jnp.concatenate([r[:, cols] for r in refs], axis=0)


def project_back(grads, weights, start, rows, kind):
    count, blocks = len(grads), len(weights)
    tok, width = grads[0].shape
    step = width // blocks
    total = tok * count
    half = total // 2

    def kernel(*refs):
        grad_refs, weight_refs = refs[:count], refs[count : count + blocks]
        mine, theirs = refs[count + blocks :]
        acc = None
        for j in range(blocks):
            left = rows_of(grad_refs, slice(j * step, (j + 1) * step))
            base = 0 if weights[j].shape[0] == rows else start
            term = mm(left, weight_refs[j][base : base + rows], NT)
            acc = term if acc is None else acc + term
        mine[...] = acc[:half]
        theirs[...] = acc[half:].astype(kind)

    return call(
        kernel,
        (jax.ShapeDtypeStruct((half, rows), F32), jax.ShapeDtypeStruct((half, rows), kind)),
        2 * total * width * rows, 2 * total * width + 2 * rows * width + 6 * half * rows,
        in_specs=[whole()] * (count + blocks), out_specs=(whole(), whole()),
    )(*grads, *weights)


def weight_terms(grads, mine, theirs, types):
    count, blocks = len(grads), len(types)
    tok, width = grads[0].shape
    rows, _ = mine.shape
    step = width // blocks
    total = tok * count

    def kernel(*refs):
        grad_refs, (a, b), outs = refs[:count], refs[count : count + 2], refs[count + 2 :]
        left = jnp.concatenate([a[...], b[...]], axis=1)
        for j in range(blocks):
            right = rows_of(grad_refs, slice(j * step, (j + 1) * step))
            outs[j][...] = mm(left, right, NN).astype(outs[j].dtype)

    return list(call(
        kernel, [jax.ShapeDtypeStruct((rows, step), t) for t in types],
        2 * total * width * rows, 2 * total * width + 4 * rows * width,
        in_specs=[whole()] * (count + 2), out_specs=[whole()] * blocks,
    )(*grads, mine, theirs))


def join_heads(chunks, cosine, sine, at):
    seq, tok = len(chunks[0]), cosine.shape[0]
    size = chunks[0][0].shape[0]
    rows = len(chunks) * size * HD

    def kernel(at_ref, cos, sin, *refs):
        ins, outs, (held, sems) = refs[:-5], refs[-5:-2], refs[-2:]
        c, s = cos[...], sin[...]
        copies = []
        for part in range(seq):
            for j in range(len(chunks)):
                src = ins[j * seq + part]
                for h in range(size):
                    first = (j * size + h) * HD
                    cols = slice(first, first + HD)
                    for i in range(2):
                        x = src[h, i].astype(F32)
                        held[i, part, :, cols] = (x * c - pltpu.roll(x, HD // 2, 1) * s).astype(BF)
                    held[2, part, :, cols] = src[h, 2]
            start = pl.multiple_of((at_ref[0] ^ part) * rows, HD)
            for i in range(3):
                copies.append(pltpu.make_async_copy(
                    held.at[i, part], outs[i].at[:, pl.ds(start, rows)], sems.at[i, part]
                ))
                copies[-1].start()
        for copy in copies:
            copy.wait()

    shape = jax.ShapeDtypeStruct((tok, rows * seq), BF)
    flat = [x for chunk in chunks for x in chunk]
    return call(
        kernel, (shape, shape, shape), 0, 12 * tok * rows * seq,
        in_specs=[smem()] + [whole()] * (2 + len(flat)), out_specs=tuple(anywhere(3)),
        scratch_shapes=[pltpu.VMEM((3, seq, tok, rows), BF), pltpu.SemaphoreType.DMA((3, seq))],
    )(at, cosine, sine, *flat)


def finish_rows(index, chunks, terms, got, into):
    rows, width = terms[0].shape
    each = len(got[0])
    count = len(terms)

    def kernel(*refs):
        held, sems, out = refs[-2], refs[-1], refs[-3]
        copies = []
        for j in range(count):
            total = refs[j][...]
            for r in refs[count + j * each : count + (j + 1) * each]:
                total = total + r[...].astype(F32)
            held[j] = total
            copies.append(pltpu.make_async_copy(
                held.at[j], out.at[pl.ds((index + j) * rows, rows)], sems.at[j]
            ))
            copies[-1].start()
        for copy in copies:
            copy.wait()

    old, flat = list(into), [g for group in got for g in group]
    return call(
        kernel, jax.ShapeDtypeStruct((rows * chunks, width), F32),
        0, 12 * count * rows * width,
        in_specs=[whole()] * (count + len(flat)) + anywhere(len(old)), out_specs=anywhere(1)[0],
        scratch_shapes=[pltpu.VMEM((count, rows, width), F32), pltpu.SemaphoreType.DMA((count,))],
        input_output_aliases={count + len(flat): 0} if old else {},
    )(*terms, *flat, *old)


def anywhere(count):
    return [pl.BlockSpec(memory_space=pl.ANY)] * count


def rotary_tables(positions):
    half = HD // 2
    frequency = 10000.0 ** (-2.0 * jnp.arange(half, dtype=F32) / HD)
    angles = positions.astype(F32)[:, None] * frequency[None, :]
    cosine, sine = jnp.cos(angles), jnp.sin(angles)
    return jnp.concatenate([cosine, cosine], 1), jnp.concatenate([-sine, sine], 1)


def shards(seq, fsdp, query_in, key_in, value_in, positions, grad_out, out_weight):
    query, key, value, grad = query_in[0], key_in[0], value_in[0], grad_out[0]
    seq_bits, clip_bits = bits_of(seq), bits_of(fsdp)
    pair = clip_bits[0]
    rest = [b for b in clip_bits if b != pair]
    order = [0]
    for bit in reversed(rest):
        order += [m | bit for m in order]
    heads = query.shape[1] // HD // seq
    chunks = next(n for n in range(CHUNKS, 0, -1) if heads % n == 0)
    size = heads // chunks
    rows = size * HD

    at = jnp.stack([lax.axis_index("seq"), lax.axis_index("fsdp")]).astype(jnp.int32)

    def send(x, axis, bit):
        n = {"seq": seq, "fsdp": fsdp}[axis]
        return lax.ppermute(x, axis, [(i, i ^ bit) for i in range(n)])

    split = split_columns(grad, fsdp, order, pair)
    own, other = split(at)
    grads = [{0: own}, {0: send(other, "fsdp", pair)}]
    for held in grads:
        for bit in reversed(seq_bits):
            for m in list(held):
                held[m | bit] = send(held[m], "seq", bit)
    sides = [held[m] for held in grads for m in range(seq)]

    weights = [{} for _ in range(chunks)]
    for bit in reversed(rest):
        arrived = send(out_weight, "fsdp", bit) if bit == rest[0] else None
        for j, held in enumerate(weights):
            if bit == rest[0]:
                for m in list(held):
                    held[m | bit] = send(held[m], "fsdp", bit)
                held[bit] = arrived
                held[0] = out_weight
            else:
                for m in list(held):
                    held[m | bit] = send(held[m], "fsdp", bit)
                piece = out_weight[j * rows : (j + 1) * rows]
                held[bit] = send(piece, "fsdp", bit)
    weights = [[held[m] for m in order] for held in weights]

    cosine, sine = rotary_tables(positions[0])
    parts = cut_heads(query, key, value, cosine, sine, at, seq, [size] * chunks)
    parts = [[p if m == 0 else send(p, "seq", m) for m, p in enumerate(c)] for c in parts]

    types = [BF if rest and m & rest[0] else F32 for m in order]
    back, sums = [], []
    for j in range(chunks):
        mine = attend(parts[j])
        theirs = send(mine, "fsdp", pair)
        terms = dict(zip(order, weight_terms(sides, mine, theirs, types)))
        last = []
        for bit in rest:
            for m in [m for m in order if m & bit and m in terms]:
                got = send(terms.pop(m).astype(BF), "fsdp", bit)
                if m == bit:
                    last.append(got)
                else:
                    terms[m ^ bit] = terms[m ^ bit] + got.astype(F32)
        sums.append((terms[0], last))

        kind = F32 if j < chunks - 1 else BF
        near, far = project_back(sides, weights[j], j * rows, rows, kind)
        far = send(far, "fsdp", pair)
        grads_back = attend_back(parts[j], near, far)
        back.append([g if m == 0 else send(g, "seq", m) for m, g in enumerate(grads_back)])

    outs = join_heads(back, cosine, sine, at)
    grad_weight = ()
    for first, stop in ((0, chunks - 1), (chunks - 1, chunks)):
        if first < stop:
            terms, got = zip(*sums[first:stop])
            grad_weight = (
                finish_rows(first, chunks, terms, got, grad_weight),
            )
    return (*(o[None] for o in outs), grad_weight[0])


def solution(mesh):
    tokens = P("fsdp", "seq", None)

    def body(*args):
        return shards(mesh.shape["seq"], mesh.shape["fsdp"], *args)

    return jax.shard_map(
        body,
        mesh=mesh,
        in_specs=(tokens, tokens, tokens, P("fsdp", "seq"), tokens, P("seq", "fsdp")),
        out_specs=(tokens, tokens, tokens, P("seq", "fsdp")),
        check_vma=False,
    )
```
